32 devices in a mesh: row: 8 (over z, core), col: 4 (over y, x).
Axes of the slice: x: 2, y: 2, z: 4, core: 2. Of those that a mesh axis runs over, the one named last changes fastest.
Arguments:
- a_blocks: bfloat16 [8, 4, 96, 128, 128], P('row', 'col'), may hold values from -0.5 to 0.5
- a_rows: int32 [8, 4, 96], P('row', 'col'), may hold values from 0 to 7, as said below
- a_cols: int32 [8, 4, 96], P('row', 'col'), may hold values from 0 to 15, as said below
- p_blocks: bfloat16 [64, 128, 256], P(('row', 'col')), may hold values from -0.5 to 0.5
- coarse_slot: int32 [8, 4, 96, 4, 4], P('row', 'col'), may hold values from 0 to 31
Outputs:
- coarse_blocks: bfloat16 [8, 32, 4096], P('row', 'col')
The draws below stay inside these ranges and needn't reach their ends.
Inputs may be any that keep to these rules, and one draw needn't show every extreme that they name: On each owner the pairs (a_rows, a_cols) of its 96 blocks are distinct. On each owner the pairs (a_rows, a_cols) of its 96 blocks are distinct.
All inputs are finite; a program needn't handle non-finite values.
Results may differ from the reference program's by a relative error of at most 0.0049.
Values may be sent and summed in bfloat16 or wider, within the bound.
No kernel may reach another device: no remote copies, remote signals or barrier semaphores. Data moves between devices by JAX's collectives and lax.ppermute only.
A program may use at most 128 MiB of HBM per device.

```python
import jax
import jax.numpy as jnp
from jax import lax

NODE = 128
AGG = 64
KP = 4
FQ = 2
KA = 96
FR = 8
FC = 16
NF = 64
KS = 32
N_ROW = 8
N_COL = 4


def pattern(key):
    folded = jax.random.fold_in(key, 7)
    device_keys = jax.random.split(folded, N_ROW * N_COL)

    def draw_one(subkey):
        shuffled = jax.random.permutation(subkey, FR * FC)
        return shuffled[:KA].astype(jnp.int32)
    return jax.vmap(draw_one)(device_keys).reshape(N_ROW, N_COL, KA)


def draw_a_rows(key, part):
    return (pattern(key) // FC).astype(jnp.int32)


def draw_a_cols(key, part):
    return (pattern(key) % FC).astype(jnp.int32)


def touch_ends(entries, rng, low, high):
    index_at = [jax.random.randint(jax.random.fold_in(rng, axis), (), 0, length) for axis, length in enumerate(entries.shape)]
    longest = entries.shape.index(max(entries.shape))
    beside = index_at[:longest] + [(index_at[longest] + 1) % entries.shape[longest]] + index_at[longest + 1:]
    return entries.at[tuple(index_at)].set(low).at[tuple(beside)].set(high)


def block_scale(rng, shape, cuts, smallest, high):
    def one(axis_at, shards_of):
        heights = jax.random.uniform(jax.random.fold_in(jax.random.fold_in(rng, 6), axis_at), (shards_of,), jnp.float32, smallest / len(cuts), high / len(cuts))
        return jnp.repeat(jnp.exp(heights), shape[axis_at] // shards_of).reshape((-1,) + (1,) * (len(shape) - axis_at - 1))

    loudness = one(*cuts[0])
    for cut in cuts[1:]:
        loudness = loudness * one(*cut)
    return loudness


def centred(stream_key, extent, spread, limit, cuts=(), kind=jnp.bfloat16):
    result = jax.random.normal(stream_key, extent, jnp.float32) * spread
    if len(cuts) > 0:
        result = block_scale(stream_key, extent, cuts, -0.22, 0.18) * result
    return jnp.clip(result, min=-limit, max=limit).astype(kind)


def setup_inputs(seed: int = 0) -> dict:
    keys = jax.random.split(jax.random.key(seed), 6)
    a_blocks = centred(keys[0], (N_ROW, N_COL, KA, NODE, NODE), NODE ** -0.5, 0.5, ((0, 8), (1, 4)))
    a_rows = draw_a_rows(jax.random.fold_in(keys[5], 71), 0)
    a_cols = draw_a_cols(jax.random.fold_in(keys[5], 71), 0)
    p_blocks = centred(keys[3], (NF, NODE, KP * AGG), NODE ** -0.5, 0.5, ((0, 32),))
    coarse_slot = touch_ends(jax.random.randint(keys[4], (N_ROW, N_COL, KA, KP, KP), 0, KS), jax.random.fold_in(keys[4], 1), 0, KS - 1).astype(jnp.int32)
    return dict(a_blocks=a_blocks, a_rows=a_rows, a_cols=a_cols, p_blocks=p_blocks, coarse_slot=coarse_slot)


def owner_terms(blocks, row_ids, col_ids, slot_ids, row_panel, column_panel):
    count = blocks.shape[0]
    group_size = 16 if count % 16 == 0 else 8 if count % 8 == 0 else 1
    groups = count // group_size
    node_width = blocks.shape[1]
    panel_width = row_panel.shape[2]
    agg_blocks = slot_ids.shape[1]
    agg_width = panel_width // agg_blocks

    def accumulate(running, batch_item):
        blk, rws, cls, sls = batch_item
        right_rows = jnp.take(column_panel, cls, axis=0)
        product = jnp.einsum("kab,kbw->kaw", blk.astype(jnp.float32), right_rows.astype(jnp.float32)).astype(jnp.bfloat16)
        left_rows = jnp.take(row_panel, rws, axis=0)
        left_split = left_rows.reshape(group_size, node_width, agg_blocks, agg_width).astype(jnp.float32)
        right_split = product.reshape(group_size, node_width, agg_blocks, agg_width).astype(jnp.float32)
        contribs = jnp.einsum("knta,knsb->ktsab", left_split, right_split)
        contribs = contribs.reshape(group_size * agg_blocks * agg_blocks, agg_width * agg_width)
        running = running.at[sls.reshape(-1)].add(contribs)
        return running, None

    items = (blocks.reshape(groups, group_size, node_width, node_width),
             row_ids.reshape(groups, group_size),
             col_ids.reshape(groups, group_size),
             slot_ids.reshape(groups, group_size, agg_blocks, agg_blocks))
    start = jnp.zeros((KS, agg_width * agg_width), jnp.float32)
    running, _ = lax.scan(accumulate, start, items)
    return running


def reference(a_blocks, a_rows, a_cols, p_blocks, coarse_slot):
    row_span = N_COL * FQ
    col_span = N_ROW * FQ

    def per_row(row_index):
        row_panel = lax.dynamic_slice_in_dim(p_blocks, row_index * row_span, row_span, 0)

        def per_col(running, col_index):
            column_panel = lax.dynamic_slice_in_dim(p_blocks, col_index * col_span, col_span, 0)
            blocks = a_blocks[row_index, col_index]
            row_ids = a_rows[row_index, col_index].astype(jnp.int32)
            col_ids = a_cols[row_index, col_index].astype(jnp.int32)
            slot_ids = coarse_slot[row_index, col_index].astype(jnp.int32)
            return running + owner_terms(blocks, row_ids, col_ids, slot_ids, row_panel, column_panel), None

        start = jnp.zeros((KS, AGG * AGG), jnp.float32)
        running, _ = lax.scan(per_col, start, jnp.arange(N_COL, dtype=jnp.int32))
        return running.astype(jnp.bfloat16)

    return lax.map(per_row, jnp.arange(N_ROW, dtype=jnp.int32))
```

```python
from functools import partial

import jax
import jax.numpy as jnp
from jax import lax
from jax.experimental import pallas as pl
from jax.experimental.pallas import tpu as pltpu
from jax.sharding import PartitionSpec as P

KS_DEV = 8
N_ACC = 4
VMEM = pl.BlockSpec(memory_space=pltpu.VMEM)
SMEM = pl.BlockSpec(memory_space=pltpu.SMEM)
F32 = jnp.float32
BF16 = jnp.bfloat16


def iota(shape, axis):
    return lax.broadcasted_iota(jnp.int32, shape, axis)


def unroll_of(count, most):
    return max(u for u in range(1, most + 1) if count % u == 0)


def left_kernel(n_parts, agg_blocks, rows_ref, *refs):
    parts, (blocks_ref, left_ref, turned) = refs[:n_parts], refs[n_parts:]
    per_part, node, width = parts[0].shape
    agg = width // agg_blocks
    half = agg // 2
    tall = agg_blocks * half
    out_row, in_col = iota((width, width), 0), iota((width, width), 1)
    within = out_row % tall
    wanted = (within // half) * agg + 2 * (within % half) + out_row // tall
    order = jnp.where(in_col == wanted, 1.0, 0.0).astype(BF16)
    me = lax.axis_index("col")
    for step, part in enumerate(parts):
        source = lax.rem(me - step + n_parts, n_parts)
        for e in range(per_part):
            turned[source * per_part + e] = lax.dot_general(
                order, part[e], (((1,), (1,)), ((), ())), preferred_element_type=F32
            ).astype(BF16)

    count = blocks_ref.shape[0]

    def one(k, _):
        both = jnp.dot(turned[rows_ref[k]], blocks_ref[k], preferred_element_type=F32).astype(BF16)
        left_ref[k, :, :node] = both[:tall]
        left_ref[k, :, node:] = both[tall:]
        return 0

    lax.fori_loop(0, count, one, 0, unroll=unroll_of(count, 8))


def sum_kernel(n_cols, fan, agg_blocks, cols_ref, slots_ref, *refs):
    n_parts = n_cols * fan
    parts, left_ref = refs[:n_parts], refs[n_parts]
    own_ref, sent_refs = refs[n_parts + 1], refs[n_parts + 2 : n_parts + 1 + n_cols]
    wide, accs = refs[n_parts + 1 + n_cols], refs[n_parts + 2 + n_cols :]
    per_part, node, width = parts[0].shape
    agg = width // agg_blocks
    half = agg // 2
    for acc in accs:
        acc[...] = jnp.zeros_like(acc)
    row = lax.axis_index("row")
    mine, line = lax.rem(row, fan), lax.div(row, fan)
    src, dst = iota((width, 2 * width), 0), iota((width, 2 * width), 1)
    spread = [
        jnp.where(dst == (src // agg) * 2 * agg + h * agg + src % agg, 1.0, 0.0).astype(BF16)
        for h in range(2)
    ]
    for g in range(fan):
        owner = lax.rem(mine - g + fan, fan)
        for step in range(n_cols):
            source = lax.rem(line - step + n_cols, n_cols)
            for e in range(per_part):
                j = (owner * n_cols + source) * per_part + e
                piece = parts[g * n_cols + step][e]
                for h in range(2):
                    wide[j, h * node : (h + 1) * node] = jnp.dot(
                        piece, spread[h], preferred_element_type=F32
                    ).astype(BF16)

    count = left_ref.shape[0]
    pairs = agg_blocks * agg_blocks

    def one(k, _):
        term = jnp.dot(left_ref[k], wide[cols_ref[k]], preferred_element_type=F32)
        for t in range(agg_blocks):
            for s in range(agg_blocks):
                slot = slots_ref[k * pairs + t * agg_blocks + s]
                acc = accs[(t * agg_blocks + s) % len(accs)]
                acc[slot] += term[t * half : (t + 1) * half, s * 2 * agg : (s + 1) * 2 * agg]
        return 0

    lax.fori_loop(0, count, one, 0, unroll=unroll_of(count, 16))

    me = lax.axis_index("col")
    for step in range(n_cols):
        first = lax.rem(me + step, n_cols) * KS_DEV
        total = accs[0][pl.ds(first, KS_DEV)]
        for acc in accs[1:]:
            total += acc[pl.ds(first, KS_DEV)]
        if step == 0:
            own_ref[...] = total
        else:
            sent_refs[step - 1][...] = total.astype(BF16)


def final_kernel(own_ref, *refs):
    got, out_ref = refs[:-1], refs[-1]
    lanes = own_ref.shape[2]
    for a in range(own_ref.shape[1]):
        total = own_ref[:, a, :]
        for part in got:
            total += part[:, a, :].astype(F32)
        out_ref[0, :, a * lanes : (a + 1) * lanes] = total.astype(BF16)


def on_device(a_blocks, a_rows, a_cols, p_blocks, coarse_slot):
    rows_total = lax.axis_size("row")
    cols_total = lax.axis_size("col")
    fan = rows_total // cols_total
    per_part, node, width = p_blocks.shape
    count = a_blocks.shape[2]
    agg_blocks = coarse_slot.shape[3]
    agg = width // agg_blocks
    both = ("row", "col")

    def shift(x, axis, d, n):
        return lax.ppermute(x, axis, [(i, (i + d) % n) for i in range(n)])

    row_parts = [p_blocks] + [shift(p_blocks, "col", d, cols_total) for d in range(1, cols_total)]
    direct = []
    for d in range(cols_total):
        pairs = []
        for c in range(cols_total):
            for f in range(fan):
                for x in range(cols_total):
                    target = ((x + d) % cols_total) * fan + f
                    pairs.append(((c * fan + f) * cols_total + x, target * cols_total + c))
        direct.append(lax.ppermute(p_blocks, both, pairs))
    col_parts = list(direct)
    for g in range(1, fan):
        swap = [(r, (r // fan) * fan + (r % fan + g) % fan) for r in range(rows_total)]
        col_parts += [lax.ppermute(part, "row", swap) for part in direct]

    left = pl.pallas_call(
        partial(left_kernel, cols_total, agg_blocks),
        out_shape=jax.ShapeDtypeStruct((count, width // 2, 2 * node), BF16),
        in_specs=[SMEM] + [VMEM] * (cols_total + 1),
        out_specs=VMEM,
        scratch_shapes=[pltpu.VMEM((per_part * cols_total, width, node), BF16)],
        name="left",
    )(a_rows.reshape(-1), *row_parts, a_blocks.reshape(a_blocks.shape[2:]))

    slot_count = KS_DEV * cols_total
    chunk = (KS_DEV, agg // 2, 2 * agg)
    sums = pl.pallas_call(
        partial(sum_kernel, cols_total, fan, agg_blocks),
        out_shape=[jax.ShapeDtypeStruct(chunk, F32)]
        + [jax.ShapeDtypeStruct(chunk, BF16)] * (cols_total - 1),
        in_specs=[SMEM] * 2 + [VMEM] * (cols_total * fan + 1),
        out_specs=[VMEM] * cols_total,
        scratch_shapes=[pltpu.VMEM((per_part * cols_total * fan, 2 * node, 2 * width), BF16)]
        + [pltpu.VMEM((slot_count,) + chunk[1:], F32)] * N_ACC,
        name="sums",
    )(a_cols.reshape(-1), coarse_slot.reshape(-1), *col_parts, left)
    got = [shift(part, "col", d, cols_total) for d, part in enumerate(sums[1:], 1)]
    return pl.pallas_call(
        final_kernel,
        out_shape=jax.ShapeDtypeStruct((1, KS_DEV, agg * agg), BF16),
        in_specs=[VMEM] * cols_total,
        out_specs=VMEM,
        name="final",
    )(sums[0], *got)


def solution(mesh):
    placed = (
        P("row", "col", None, None, None),
        P("row", "col", None),
        P("row", "col", None),
        P(("row", "col"), None, None),
        P("row", "col", None, None, None),
    )
    return jax.shard_map(
        on_device, mesh=mesh, in_specs=placed, out_specs=P("row", "col", None), check_vma=False
    )
```

```python
from functools import partial

import jax
import jax.numpy as jnp
from jax import lax
from jax.experimental import pallas as pl
from jax.experimental.pallas import tpu as pltpu
from jax.sharding import PartitionSpec as P


KS_DEV = 8
N_ACC = 4
SHIFT = 16
BIG = 1 << SHIFT
VMEM = pl.BlockSpec(memory_space=pltpu.VMEM)
SMEM = pl.BlockSpec(memory_space=pltpu.SMEM)
HBM = pl.BlockSpec(memory_space=pltpu.HBM)
F32 = jnp.float32
BF16 = jnp.bfloat16


def in_hbm(x):
    return pltpu.with_memory_space_constraint(x, pltpu.HBM)


def iota(shape, axis):
    return lax.broadcasted_iota(jnp.int32, shape, axis)


def partner(i, d, n):
    return i ^ d if n & (n - 1) == 0 else (n - i + d) % n


def step_of(q, n):
    return (q + n - 1) % n


def unroll_of(count, most):
    return max(u for u in range(1, most + 1) if count % u == 0)


def left_kernel(n_cols, fan, agg_blocks, rows_hbm, cols_hbm, piece_hbm, *refs):
    got, rest = refs[: n_cols - 1], refs[n_cols - 1 :]
    blocks_hbm, left_ref, table_ref, turned, own, blocks_ref, rows_ref, cols_ref = rest[:8]
    block_sems, own_sem, row_sem, col_sem = rest[8:]
    parts = (own,) + got
    per_part, node, width = own.shape
    count = blocks_ref.shape[0]
    n_chunks = block_sems.shape[0]
    size = count // n_chunks
    chunks = [
        pltpu.make_async_copy(
            blocks_hbm.at[pl.ds(c * size, size)], blocks_ref.at[pl.ds(c * size, size)], block_sems.at[c]
        )
        for c in range(n_chunks)
    ]
    get_rows = pltpu.make_async_copy(rows_hbm, rows_ref, row_sem)
    get_cols = pltpu.make_async_copy(cols_hbm, cols_ref, col_sem)
    get_own = pltpu.make_async_copy(piece_hbm, own, own_sem)
    get_rows.start()
    get_cols.start()
    get_own.start()
    for chunk in chunks:
        chunk.start()

    agg = width // agg_blocks
    half = agg // 2
    tall = agg_blocks * half
    out_row, in_col = iota((width, width), 0), iota((width, width), 1)
    within = out_row % tall
    wanted = (within // half) * agg + 2 * (within % half) + out_row // tall
    order = jnp.where(in_col == wanted, 1.0, 0.0).astype(BF16)
    me = lax.axis_index("col")
    for step in list(range(1, n_cols)) + [0]:
        if step == 0:
            get_own.wait()
        source = lax.rem(me - step + n_cols, n_cols)
        for e in range(per_part):
            turned[source * per_part + e] = lax.dot_general(
                order, parts[step][e], (((1,), (1,)), ((), ())), preferred_element_type=F32
            ).astype(BF16)

    get_rows.wait()
    get_cols.wait()
    row = lax.axis_index("row")
    mine, line = lax.rem(row, fan), lax.div(row, fan)
    table_ref[count] = 0

    def enter(k, n):
        j = cols_ref[k]
        e, source, owner = lax.rem(j, per_part), lax.rem(lax.div(j, per_part), n_cols), lax.div(j, n_cols * per_part)
        q = lax.rem(line - source + n_cols + 1, n_cols)
        g = lax.rem(mine - owner + fan, fan)
        early = (g == 0) & (q < n_cols - 1)
        part = jnp.where(early, q, jnp.where(g == 0, 0, 1 + (g - 1) * n_cols + q))
        place = jnp.where(early, n, count - 1 - (k - n))
        table_ref[place] = k + (part * per_part + e + 1) * BIG
        return n + jnp.where(early, 1, 0)

    unroll = unroll_of(size, 8)

    def some(b, n):
        for u in range(unroll):
            k = b * unroll + u
            both = jnp.dot(turned[rows_ref[k]], blocks_ref[k], preferred_element_type=F32).astype(BF16)
            left_ref[k, :, :node] = both[:tall]
            left_ref[k, :, node:] = both[tall:]
            n = enter(k, n)
        return n

    n = jnp.int32(0)
    for c, chunk in enumerate(chunks):
        chunk.wait()
        n = lax.fori_loop(c * size // unroll, (c + 1) * size // unroll, some, n)
    table_ref[count + 1] = n


def spread(piece, agg_blocks):
    node, width = piece.shape
    agg = width // agg_blocks
    low = iota((node, 2 * agg), 1) < agg
    zero = jnp.zeros((node, 2 * agg), BF16)
    top, bottom = [], []
    for v in range(agg_blocks // 2):
        straight = piece[:, v * 2 * agg : (v + 1) * 2 * agg]
        turned = pltpu.roll(straight.astype(F32), agg, 1).astype(BF16)
        top += [jnp.where(low, straight, zero), jnp.where(low, turned, zero)]
        bottom += [jnp.where(low, zero, turned), jnp.where(low, zero, straight)]
    return top, bottom


def sum_kernel(n_parts, early, agg_blocks, unroll, table_in, slots_hbm, *refs):
    parts, left_ref, rest = refs[:n_parts], refs[n_parts], refs[n_parts + 1 :]
    before = None
    if not early:
        before, rest = rest[0], rest[1:]
    outs, rest = rest[: -6 - N_ACC], rest[-6 - N_ACC :]
    table_ref, slots_ref, table_sem, slot_sem, wide, turn = rest[:6]
    accs = rest[6:]
    count = left_ref.shape[0]
    get_slots = pltpu.make_async_copy(slots_hbm, slots_ref, slot_sem)
    get_slots.start()
    get_table = pltpu.make_async_copy(table_in, table_ref, table_sem)
    get_table.start()
    per_part, node, width = parts[0].shape
    agg = width // agg_blocks
    half = agg // 2
    lanes = 2 * agg
    for i, acc in enumerate(accs):
        acc[...] = before[...] if i == 0 and before is not None else jnp.zeros_like(acc)
    wide[0] = jnp.zeros_like(wide[0])
    for q, part in enumerate(parts):
        for e in range(per_part):
            for h, blocks in enumerate(spread(part[e], agg_blocks)):
                for s, block in enumerate(blocks):
                    wide[1 + q * per_part + e, h * node : (h + 1) * node, s * lanes : (s + 1) * lanes] = block

    get_table.wait()
    get_slots.wait()
    n = table_ref[count + 1] if early else count - table_ref[count + 1]

    def some(b, _):
        for u in range(unroll):
            p = b * unroll + u
            entry = table_ref[jnp.where(p < n, p if early else count - 1 - p, count)]
            k = entry & (BIG - 1)
            term = jnp.dot(left_ref[k], wide[lax.shift_right_logical(entry, SHIFT)], preferred_element_type=F32)
            for i in range(agg_blocks * agg_blocks):
                t, s = divmod(i, agg_blocks)
                slot = slots_ref[t, s, k]
                accs[i % N_ACC][slot] += term[t * half : (t + 1) * half, s * lanes : (s + 1) * lanes]
        return 0

    lax.fori_loop(0, lax.div(n + unroll - 1, unroll), some, 0)

    if early:
        total = accs[0][...]
        for acc in accs[1:]:
            total += acc[...]
        outs[0][...] = total
        return
    me = lax.axis_index("col")
    for step, out in enumerate(outs):
        slots = pl.ds(partner(me, step, len(outs)) * KS_DEV, KS_DEV)
        total = accs[0][slots]
        for acc in accs[1:]:
            total += acc[slots]
        turn[step] = total.reshape(KS_DEV * half, lanes)
        for a in range(half):
            out[:, a * lanes : (a + 1) * lanes] = turn[step, pl.ds(a, KS_DEV, stride=half), :].astype(out.dtype)


def on_device(a_blocks, a_rows, a_cols, p_blocks, coarse_slot):
    rows_total = lax.axis_size("row")
    cols_total = lax.axis_size("col")
    fan = rows_total // cols_total
    per_part, node, width = p_blocks.shape
    count = a_blocks.shape[2]
    agg_blocks = coarse_slot.shape[3]
    agg = width // agg_blocks

    def shift(x, to):
        return lax.ppermute(x, "col", [(i, to(i)) for i in range(cols_total)])

    def across(x, g):
        swap = [(r, (r // fan) * fan + (r % fan + g) % fan) for r in range(rows_total)]
        return lax.ppermute(x, "row", swap)

    row_parts = [p_blocks]
    for d in range(1, cols_total):
        row_parts.append(shift(p_blocks, lambda i, d=d: (i + d) % cols_total))
    direct = []
    for q in range(cols_total):
        pairs = []
        for c in range(cols_total):
            for f in range(fan):
                for x in range(cols_total):
                    target = ((x + step_of(q, cols_total)) % cols_total) * fan + f
                    pairs.append(((c * fan + f) * cols_total + x, target * cols_total + c))
        direct.append(lax.ppermute(p_blocks, ("row", "col"), pairs))
    early, late = direct[:-1], direct[-1:]
    for g in range(1, fan):
        late += [across(part, g) for part in direct]

    rows, cols = in_hbm(a_rows.reshape(-1)), in_hbm(a_cols.reshape(-1))
    slots = in_hbm(coarse_slot.transpose(0, 1, 3, 4, 2).reshape(agg_blocks, agg_blocks, count))
    table = jax.ShapeDtypeStruct((count + 2,), jnp.int32)
    left, table_in = pl.pallas_call(
        partial(left_kernel, cols_total, fan, agg_blocks),
        out_shape=[jax.ShapeDtypeStruct((count, width // 2, 2 * node), BF16), table],
        in_specs=[HBM] * 3 + [VMEM] * (cols_total - 1) + [HBM],
        out_specs=[VMEM, SMEM],
        scratch_shapes=[
            pltpu.VMEM((per_part * cols_total, width, node), BF16),
            pltpu.VMEM((per_part, node, width), BF16),
            pltpu.VMEM((count, node, node), BF16),
            pltpu.SMEM((count,), jnp.int32),
            pltpu.SMEM((count,), jnp.int32),
            pltpu.SemaphoreType.DMA((unroll_of(count, 4),)),
        ]
        + [pltpu.SemaphoreType.DMA] * 3,
        compiler_params=pltpu.CompilerParams(vmem_limit_bytes=16 << 20),
        cost_estimate=pl.CostEstimate(
            flops=2 * count * width * node * node, bytes_accessed=20 << 20, transcendentals=0
        ),
        name="left",
    )(rows, cols, in_hbm(p_blocks), *row_parts[1:], in_hbm(a_blocks.reshape(a_blocks.shape[2:])))

    chunk = (KS_DEV, agg * agg)
    block = (agg // 2, 2 * agg)
    slot_count = KS_DEV * cols_total
    sums = []
    for stage, parts in enumerate((early, late)):
        if stage:
            outs = [jax.ShapeDtypeStruct(chunk, BF16 if q else F32) for q in range(cols_total)]
        else:
            outs = [jax.ShapeDtypeStruct((slot_count,) + block, F32)]
        sums = pl.pallas_call(
            partial(sum_kernel, len(parts), not stage, agg_blocks, 12 if stage else 8),
            out_shape=outs,
            in_specs=[pl.BlockSpec(memory_space=pl.ANY), HBM] + [VMEM] * (len(parts) + 1 + stage),
            out_specs=[VMEM] * len(outs),
            scratch_shapes=[
                pltpu.SMEM(table.shape, jnp.int32),
                pltpu.SMEM((agg_blocks, agg_blocks, count), jnp.int32),
                pltpu.SemaphoreType.DMA,
                pltpu.SemaphoreType.DMA,
                pltpu.VMEM((1 + len(parts) * per_part, 2 * node, 2 * width), BF16),
                pltpu.VMEM((cols_total, KS_DEV * block[0], block[1]), F32),
            ]
            + [pltpu.VMEM((slot_count,) + block, F32)] * N_ACC,
            compiler_params=pltpu.CompilerParams(vmem_limit_bytes=36 << 20),
            cost_estimate=pl.CostEstimate(
                flops=4 * count * width * node * node, bytes_accessed=10 << 20, transcendentals=0
            ),
        )(table_in, slots, *parts, left, *sums)
    total = sums[0]
    for d in range(1, cols_total):
        total += shift(sums[d], lambda i, d=d: partner(i, d, cols_total)).astype(F32)
    return total.astype(BF16)[None]


def solution(mesh):
    placed = (
        P("row", "col", None, None, None),
        P("row", "col", None),
        P("row", "col", None),
        P(("row", "col"), None, None),
        P("row", "col", None, None, None),
    )

    return jax.shard_map(on_device, mesh=mesh, in_specs=placed, out_specs=P("row", "col", None), check_vma=False)
```

```python
from functools import partial

import jax
import jax.numpy as jnp
from jax import lax
from jax.experimental import pallas as pl
from jax.experimental.pallas import tpu as pltpu
from jax.sharding import PartitionSpec as P


KS_DEV = 8
N_ACC = 4
SHIFT = 16
BIG = 1 << SHIFT
VMEM = pl.BlockSpec(memory_space=pltpu.VMEM)
SMEM = pl.BlockSpec(memory_space=pltpu.SMEM)
HBM = pl.BlockSpec(memory_space=pltpu.HBM)
F32 = jnp.float32
BF16 = jnp.bfloat16


def in_hbm(x):
    return pltpu.with_memory_space_constraint(x, pltpu.HBM)


def iota(shape, axis):
    return lax.broadcasted_iota(jnp.int32, shape, axis)


def partner(i, d, n):
    return i ^ d if n & (n - 1) == 0 else (n - i + d) % n


def hop(x, d, n):
    return x ^ d if n & (n - 1) == 0 else (2 * n - x + d) % n


def unroll_of(count, most):
    return max(u for u in range(1, most + 1) if count % u == 0)


def stage_kernel(blocks_hbm, blocks_ref, sem):
    copy = pltpu.make_async_copy(blocks_hbm, blocks_ref, sem)
    copy.start()
    copy.wait()


def left_kernel(n_cols, fan, agg_blocks, rows_hbm, cols_hbm, piece_hbm, *refs):
    got, rest = refs[: n_cols - 1], refs[n_cols - 1 :]
    blocks_ref, left_ref, table_ref, turned, own, rows_ref, cols_ref, own_sem, row_sem, col_sem = rest
    parts = (own,) + got
    per_part, node, width = own.shape
    count = blocks_ref.shape[0]
    get_rows = pltpu.make_async_copy(rows_hbm, rows_ref, row_sem)
    get_own = pltpu.make_async_copy(piece_hbm, own, own_sem)
    get_cols = pltpu.make_async_copy(cols_hbm, cols_ref, col_sem)
    get_rows.start()
    get_cols.start()
    get_own.start()

    agg = width // agg_blocks
    half = agg // 2
    tall = agg_blocks * half
    out_row, in_col = iota((width, width), 0), iota((width, width), 1)
    within = out_row % tall
    wanted = (within // half) * agg + 2 * (within % half) + out_row // tall
    order = jnp.where(in_col == wanted, 1.0, 0.0).astype(BF16)
    me = lax.axis_index("col")
    for step in list(range(1, n_cols)) + [0]:
        if step == 0:
            get_own.wait()
        source = lax.rem(me - step + n_cols, n_cols)
        for e in range(per_part):
            turned[source * per_part + e] = lax.dot_general(
                order, parts[step][e], (((1,), (1,)), ((), ())), preferred_element_type=F32
            ).astype(BF16)

    get_rows.wait()
    row = lax.axis_index("row")
    mine, line = lax.rem(row, fan), lax.div(row, fan)
    steps = n_cols // fan
    table_ref[count] = 0
    get_cols.wait()

    def enter(k, n):
        j = cols_ref[k]
        e, source, owner = lax.rem(j, per_part), lax.rem(lax.div(j, per_part), n_cols), lax.div(j, n_cols * per_part)
        away = hop(source, line, n_cols) if n_cols & (n_cols - 1) == 0 else lax.rem(source + line, n_cols)
        via, q = lax.div(away, steps), steps - 1 - lax.rem(away, steps)
        g = lax.rem(mine - via + fan, fan)
        early = q < (steps + 1) // 2
        part = jnp.where(early, q, q - (steps + 1) // 2) * fan + g
        spot = (part * fan + lax.rem(via - owner + fan, fan)) * per_part + e
        table_ref[jnp.where(early, n, count - 1 - (k - n))] = k + (spot + 1) * BIG
        return n + jnp.where(early, 1, 0)

    def one(k, n):
        both = jnp.dot(turned[rows_ref[k]], blocks_ref[k], preferred_element_type=F32).astype(BF16)
        left_ref[k, :, :node] = both[:tall]
        left_ref[k, :, node:] = both[tall:]
        return enter(k, n)

    table_ref[count + 1] = lax.fori_loop(0, count, one, jnp.int32(0), unroll=unroll_of(count, 16))


def spread(piece, agg_blocks):
    node, width = piece.shape
    agg = width // agg_blocks
    low = iota((node, 2 * agg), 1) < agg
    zero = jnp.zeros((node, 2 * agg), BF16)
    top, bottom = [], []
    for v in range(agg_blocks // 2):
        straight = piece[:, v * 2 * agg : (v + 1) * 2 * agg]
        turned = pltpu.roll(straight.astype(F32), agg, 1).astype(BF16)
        top += [jnp.where(low, straight, zero), jnp.where(low, turned, zero)]
        bottom += [jnp.where(low, zero, turned), jnp.where(low, zero, straight)]
    return top, bottom


def sum_kernel(n_parts, early, agg_blocks, unroll, table_in, slots_hbm, *refs):
    parts, left_ref, rest = refs[:n_parts], refs[n_parts], refs[n_parts + 1 :]
    before = None
    if not early:
        before, rest = rest[0], rest[1:]
    outs, rest = rest[: -6 - N_ACC], rest[-6 - N_ACC :]
    table_ref, slots_ref, table_sem, slot_sem, wide, turn = rest[:6]
    accs = rest[6:]
    count = left_ref.shape[0]
    get_slots = pltpu.make_async_copy(slots_hbm, slots_ref, slot_sem)
    get_slots.start()
    get_table = pltpu.make_async_copy(table_in, table_ref, table_sem)
    get_table.start()
    per_part, node, width = parts[0].shape
    agg = width // agg_blocks
    half = agg // 2
    lanes = 2 * agg
    for i, acc in enumerate(accs):
        acc[...] = before[...] if i == 0 and before is not None else jnp.zeros_like(acc)
    wide[0] = jnp.zeros_like(wide[0])
    for q, part in enumerate(parts):
        for e in range(per_part):
            for h, blocks in enumerate(spread(part[e], agg_blocks)):
                for s, block in enumerate(blocks):
                    wide[1 + q * per_part + e, h * node : (h + 1) * node, s * lanes : (s + 1) * lanes] = block

    get_table.wait()
    get_slots.wait()
    n = table_ref[count + 1] if early else count - table_ref[count + 1]

    def some(b, _):
        for u in range(unroll):
            p = b * unroll + u
            entry = table_ref[jnp.where(p < n, p if early else count - 1 - p, count)]
            k = entry & (BIG - 1)
            term = jnp.dot(left_ref[k], wide[lax.shift_right_logical(entry, SHIFT)], preferred_element_type=F32)
            for i in range(agg_blocks * agg_blocks):
                t, s = divmod(i, agg_blocks)
                slot = slots_ref[t, s, k]
                accs[i % N_ACC][slot] += term[t * half : (t + 1) * half, s * lanes : (s + 1) * lanes]
        return 0

    lax.fori_loop(0, lax.div(n + unroll - 1, unroll), some, 0)

    if early:
        total = accs[0][...]
        for acc in accs[1:]:
            total += acc[...]
        outs[0][...] = total
        return
    me = lax.axis_index("col")
    for step, out in enumerate(outs):
        slots = pl.ds(partner(me, step, len(outs)) * KS_DEV, KS_DEV)
        total = accs[0][slots]
        for acc in accs[1:]:
            total += acc[slots]
        turn[step] = total.reshape(KS_DEV * half, lanes)
        for a in range(half):
            out[:, a * lanes : (a + 1) * lanes] = turn[step, pl.ds(a, KS_DEV, stride=half), :].astype(out.dtype)


def on_device(a_blocks, a_rows, a_cols, p_blocks, coarse_slot):
    rows_total = lax.axis_size("row")
    cols_total = lax.axis_size("col")
    fan = rows_total // cols_total
    per_part, node, width = p_blocks.shape
    count = a_blocks.shape[2]
    agg_blocks = coarse_slot.shape[3]
    agg = width // agg_blocks

    def shift(x, to):
        return lax.ppermute(x, "col", [(i, to(i)) for i in range(cols_total)])

    def across(x, g):
        swap = [(r, (r // fan) * fan + (r % fan + g) % fan) for r in range(rows_total)]
        return lax.ppermute(x, "row", swap)

    row_parts = [p_blocks]
    for d in range(1, cols_total):
        row_parts.append(shift(p_blocks, lambda i, d=d: (i + d) % cols_total))
    chip = jnp.concatenate([p_blocks] + [across(p_blocks, g) for g in range(1, fan)])
    steps = cols_total // fan
    stages = ([], [])
    for q in range(steps):
        pairs = []
        for c in range(cols_total):
            for f in range(fan):
                for x in range(cols_total):
                    target = hop(x, steps - 1 - q + steps * f, cols_total) * fan + f
                    pairs.append(((c * fan + f) * cols_total + x, target * cols_total + c))
        part = lax.ppermute(chip, ("row", "col"), pairs)
        stages[q >= (steps + 1) // 2].extend([part] + [across(part, g) for g in range(1, fan)])

    rows, cols = in_hbm(a_rows.reshape(-1)), in_hbm(a_cols.reshape(-1))
    slots = in_hbm(coarse_slot.transpose(0, 1, 3, 4, 2).reshape(agg_blocks, agg_blocks, count))
    table = jax.ShapeDtypeStruct((count + 2,), jnp.int32)
    blocks = jax.ShapeDtypeStruct((count, node, node), BF16)
    staged = pl.pallas_call(
        stage_kernel,
        out_shape=blocks,
        in_specs=[HBM],
        out_specs=VMEM,
        scratch_shapes=[pltpu.SemaphoreType.DMA],
        compiler_params=pltpu.CompilerParams(vmem_limit_bytes=16 << 20),
        cost_estimate=pl.CostEstimate(flops=0, bytes_accessed=8 << 20, transcendentals=0),
        name="stage",
    )(in_hbm(a_blocks.reshape(blocks.shape)))
    left, table_in = pl.pallas_call(
        partial(left_kernel, cols_total, fan, agg_blocks),
        out_shape=[jax.ShapeDtypeStruct((count, width // 2, 2 * node), BF16), table],
        in_specs=[HBM] * 3 + [VMEM] * cols_total,
        out_specs=[VMEM, SMEM],
        scratch_shapes=[
            pltpu.VMEM((per_part * cols_total, width, node), BF16),
            pltpu.VMEM((per_part, node, width), BF16),
            pltpu.SMEM((count,), jnp.int32),
            pltpu.SMEM((count,), jnp.int32),
            pltpu.SemaphoreType.DMA,
            pltpu.SemaphoreType.DMA,
            pltpu.SemaphoreType.DMA,
        ],
        compiler_params=pltpu.CompilerParams(vmem_limit_bytes=16 << 20),
        cost_estimate=pl.CostEstimate(
            flops=2 * count * width * node * node, bytes_accessed=10 << 20, transcendentals=0
        ),
        name="left",
    )(rows, cols, in_hbm(p_blocks), *row_parts[1:], staged)

    chunk = (KS_DEV, agg * agg)
    block = (agg // 2, 2 * agg)
    slot_count = KS_DEV * cols_total
    sums = []
    for stage, parts in enumerate(stages):
        if stage:
            outs = [jax.ShapeDtypeStruct(chunk, BF16 if q else F32) for q in range(cols_total)]
        else:
            outs = [jax.ShapeDtypeStruct((slot_count,) + block, F32)]
        sums = pl.pallas_call(
            partial(sum_kernel, len(parts), not stage, agg_blocks, 12),
            out_shape=outs,
            in_specs=[pl.BlockSpec(memory_space=pl.ANY), HBM] + [VMEM] * (len(parts) + 1 + stage),
            out_specs=[VMEM] * len(outs),
            scratch_shapes=[
                pltpu.SMEM(table.shape, jnp.int32),
                pltpu.SMEM((agg_blocks, agg_blocks, count), jnp.int32),
                pltpu.SemaphoreType.DMA,
                pltpu.SemaphoreType.DMA,
                pltpu.VMEM((1 + len(parts) * fan * per_part, 2 * node, 2 * width), BF16),
                pltpu.VMEM((cols_total, KS_DEV * block[0], block[1]), F32),
            ]
            + [pltpu.VMEM((slot_count,) + block, F32)] * N_ACC,
            compiler_params=pltpu.CompilerParams(vmem_limit_bytes=36 << 20),
            cost_estimate=pl.CostEstimate(
                flops=4 * count * width * node * node, bytes_accessed=10 << 20, transcendentals=0
            ),
        )(table_in, slots, *parts, left, *sums)
    total = sums[0]
    for d in range(1, cols_total):
        total += shift(sums[d], lambda i, d=d: partner(i, d, cols_total)).astype(F32)
    return total.astype(BF16)[None]


def solution(mesh):
    placed = (
        P("row", "col", None, None, None),
        P("row", "col", None),
        P("row", "col", None),
        P(("row", "col"), None, None),
        P("row", "col", None, None, None),
    )

    return jax.shard_map(on_device, mesh=mesh, in_specs=placed, out_specs=P("row", "col", None), check_vma=False)
```

```python
from functools import partial

import jax
import jax.numpy as jnp
from jax import lax
from jax.experimental import pallas as pl
from jax.experimental.pallas import tpu as pltpu
from jax.sharding import PartitionSpec as P


KS_DEV = 8
N_ACC = 4
SHIFT = 16
BIG = 1 << SHIFT
VMEM = pl.BlockSpec(memory_space=pltpu.VMEM)
SMEM = pl.BlockSpec(memory_space=pltpu.SMEM)
HBM = pl.BlockSpec(memory_space=pltpu.HBM)
F32 = jnp.float32
BF16 = jnp.bfloat16


def in_hbm(x):
    return pltpu.with_memory_space_constraint(x, pltpu.HBM)


def iota(shape, axis):
    return lax.broadcasted_iota(jnp.int32, shape, axis)


def partner(i, d, n):
    return i ^ d if n & (n - 1) == 0 else (n - i + d) % n


def hop(x, d, n):
    return x ^ d if n & (n - 1) == 0 else (2 * n - x + d) % n


def unroll_of(count, most):
    return max(u for u in range(1, most + 1) if count % u == 0)


def stage_kernel(blocks_hbm, blocks_ref, sem):
    copy = pltpu.make_async_copy(blocks_hbm, blocks_ref, sem)
    copy.start()
    copy.wait()


def left_kernel(n_cols, fan, agg_blocks, rows_hbm, cols_hbm, piece_hbm, *refs):
    got, rest = refs[: n_cols - 1], refs[n_cols - 1 :]
    blocks_ref, left_ref, table_ref, turned, own, rows_ref, cols_ref, own_sem, row_sem, col_sem = rest
    parts = (own,) + got
    per_part, node, width = own.shape
    count = blocks_ref.shape[0]
    get_rows = pltpu.make_async_copy(rows_hbm, rows_ref, row_sem)
    get_own = pltpu.make_async_copy(piece_hbm, own, own_sem)
    get_cols = pltpu.make_async_copy(cols_hbm, cols_ref, col_sem)
    get_rows.start()
    get_cols.start()
    get_own.start()

    agg = width // agg_blocks
    half = agg // 2
    tall = agg_blocks * half
    out_row, in_col = iota((width, width), 0), iota((width, width), 1)
    within = out_row % tall
    wanted = (within // half) * agg + 2 * (within % half) + out_row // tall
    order = jnp.where(in_col == wanted, 1.0, 0.0).astype(BF16)
    me = lax.axis_index("col")
    for step in list(range(1, n_cols)) + [0]:
        if step == 0:
            get_own.wait()
        source = lax.rem(me - step + n_cols, n_cols)
        for e in range(per_part):
            turned[source * per_part + e] = lax.dot_general(
                order, parts[step][e], (((1,), (1,)), ((), ())), preferred_element_type=F32
            ).astype(BF16)

    get_rows.wait()
    row = lax.axis_index("row")
    mine, line = lax.rem(row, fan), lax.div(row, fan)
    steps = n_cols // fan
    table_ref[count] = 0
    get_cols.wait()

    def enter(k, n):
        j = cols_ref[k]
        e, source, owner = lax.rem(j, per_part), lax.rem(lax.div(j, per_part), n_cols), lax.div(j, n_cols * per_part)
        away = hop(source, line, n_cols) if n_cols & (n_cols - 1) == 0 else lax.rem(source + line, n_cols)
        via, q = lax.div(away, steps), steps - 1 - lax.rem(away, steps)
        g = lax.rem(mine - via + fan, fan)
        early = q < (steps + 1) // 2
        part = jnp.where(early, q, q - (steps + 1) // 2) * fan + g
        spot = (part * fan + lax.rem(via - owner + fan, fan)) * per_part + e
        table_ref[jnp.where(early, n, count - 1 - (k - n))] = k + (spot + 1) * BIG
        return n + jnp.where(early, 1, 0)

    def one(k, n):
        both = jnp.dot(turned[rows_ref[k]], blocks_ref[k], preferred_element_type=F32).astype(BF16)
        left_ref[k, :, :node] = both[:tall]
        left_ref[k, :, node:] = both[tall:]
        return enter(k, n)

    table_ref[count + 1] = lax.fori_loop(0, count, one, jnp.int32(0), unroll=unroll_of(count, 16))


def spread(piece, agg_blocks):
    node, width = piece.shape
    agg = width // agg_blocks
    low = iota((node, 2 * agg), 1) < agg
    zero = jnp.zeros((node, 2 * agg), BF16)
    top, bottom = [], []
    for v in range(agg_blocks // 2):
        straight = piece[:, v * 2 * agg : (v + 1) * 2 * agg]
        turned = pltpu.roll(straight, agg, 1)
        top += [jnp.where(low, straight, zero), jnp.where(low, turned, zero)]
        bottom += [jnp.where(low, zero, turned), jnp.where(low, zero, straight)]
    return top, bottom


def sum_kernel(n_parts, early, agg_blocks, unroll, table_in, slots_hbm, *refs):
    parts, left_ref, rest = refs[:n_parts], refs[n_parts], refs[n_parts + 1 :]
    before = None
    if not early:
        before, rest = rest[0], rest[1:]
    outs, rest = rest[: -5 - N_ACC], rest[-5 - N_ACC :]
    table_ref, slots_ref, table_sem, slot_sem, wide = rest[:5]
    accs = rest[5:]
    count = left_ref.shape[0]
    get_slots = pltpu.make_async_copy(slots_hbm, slots_ref, slot_sem)
    get_slots.start()
    get_table = pltpu.make_async_copy(table_in, table_ref, table_sem)
    get_table.start()
    per_part, node, width = parts[0].shape
    agg = width // agg_blocks
    half = agg // 2
    lanes = 2 * agg
    for i, acc in enumerate(accs):
        acc[...] = before[...] if i == 0 and before is not None else jnp.zeros_like(acc)
    wide[0] = jnp.zeros_like(wide[0])
    for q, part in enumerate(parts):
        for e in range(per_part):
            for h, blocks in enumerate(spread(part[e], agg_blocks)):
                for s, block in enumerate(blocks):
                    wide[1 + q * per_part + e, h * node : (h + 1) * node, s * lanes : (s + 1) * lanes] = block

    get_table.wait()
    get_slots.wait()
    n = table_ref[count + 1] if early else count - table_ref[count + 1]

    def some(b, _):
        for u in range(unroll):
            p = b * unroll + u
            entry = table_ref[jnp.where(p < n, p if early else count - 1 - p, count)]
            k = entry & (BIG - 1)
            term = jnp.dot(left_ref[k], wide[lax.shift_right_logical(entry, SHIFT)], preferred_element_type=F32)
            for i in range(agg_blocks * agg_blocks):
                t, s = divmod(i, agg_blocks)
                slot = slots_ref[t, s, k]
                accs[i % N_ACC][slot] += term[t * half : (t + 1) * half, s * lanes : (s + 1) * lanes]
        return 0

    lax.fori_loop(0, lax.div(n + unroll - 1, unroll), some, 0)

    if early:
        total = accs[0][...]
        for acc in accs[1:]:
            total += acc[...]
        outs[0][...] = total
        return
    me = lax.axis_index("col")
    for step, out in enumerate(outs):
        slots = pl.ds(partner(me, step, len(outs)) * KS_DEV, KS_DEV)
        total = accs[0][slots]
        for acc in accs[1:]:
            total += acc[slots]
        across_slots = jnp.swapaxes(total, 0, 1)
        for a in range(half):
            out[:, a * lanes : (a + 1) * lanes] = across_slots[a].astype(out.dtype)


def on_device(a_blocks, a_rows, a_cols, p_blocks, coarse_slot):
    rows_total = lax.axis_size("row")
    cols_total = lax.axis_size("col")
    fan = rows_total // cols_total
    per_part, node, width = p_blocks.shape
    count = a_blocks.shape[2]
    agg_blocks = coarse_slot.shape[3]
    agg = width // agg_blocks

    def shift(x, to):
        return lax.ppermute(x, "col", [(i, to(i)) for i in range(cols_total)])

    def across(x, g):
        swap = [(r, (r // fan) * fan + (r % fan + g) % fan) for r in range(rows_total)]
        return lax.ppermute(x, "row", swap)

    row_parts = [p_blocks]
    for d in range(1, cols_total):
        row_parts.append(shift(p_blocks, lambda i, d=d: (i + d) % cols_total))
    chip = jnp.concatenate([p_blocks] + [across(p_blocks, g) for g in range(1, fan)])
    steps = cols_total // fan
    stages = ([], [])
    for q in range(steps):
        pairs = []
        for c in range(cols_total):
            for f in range(fan):
                for x in range(cols_total):
                    target = hop(x, steps - 1 - q + steps * f, cols_total) * fan + f
                    pairs.append(((c * fan + f) * cols_total + x, target * cols_total + c))
        part = lax.ppermute(chip, ("row", "col"), pairs)
        stages[q >= (steps + 1) // 2].extend([part] + [across(part, g) for g in range(1, fan)])

    rows, cols = in_hbm(a_rows.reshape(-1)), in_hbm(a_cols.reshape(-1))
    slots = in_hbm(coarse_slot.transpose(0, 1, 3, 4, 2).reshape(agg_blocks, agg_blocks, count))
    table = jax.ShapeDtypeStruct((count + 2,), jnp.int32)
    blocks = jax.ShapeDtypeStruct((count, node, node), BF16)
    staged = pl.pallas_call(
        stage_kernel,
        out_shape=blocks,
        in_specs=[HBM],
        out_specs=VMEM,
        scratch_shapes=[pltpu.SemaphoreType.DMA],
        compiler_params=pltpu.CompilerParams(vmem_limit_bytes=16 << 20),
        cost_estimate=pl.CostEstimate(flops=0, bytes_accessed=8 << 20, transcendentals=0),
        name="stage",
    )(in_hbm(a_blocks.reshape(blocks.shape)))
    left, table_in = pl.pallas_call(
        partial(left_kernel, cols_total, fan, agg_blocks),
        out_shape=[jax.ShapeDtypeStruct((count, width // 2, 2 * node), BF16), table],
        in_specs=[HBM] * 3 + [VMEM] * cols_total,
        out_specs=[VMEM, SMEM],
        scratch_shapes=[
            pltpu.VMEM((per_part * cols_total, width, node), BF16),
            pltpu.VMEM((per_part, node, width), BF16),
            pltpu.SMEM((count,), jnp.int32),
            pltpu.SMEM((count,), jnp.int32),
            pltpu.SemaphoreType.DMA,
            pltpu.SemaphoreType.DMA,
            pltpu.SemaphoreType.DMA,
        ],
        compiler_params=pltpu.CompilerParams(vmem_limit_bytes=16 << 20),
        cost_estimate=pl.CostEstimate(
            flops=2 * count * width * node * node, bytes_accessed=10 << 20, transcendentals=0
        ),
        name="left",
    )(rows, cols, in_hbm(p_blocks), *row_parts[1:], staged)

    chunk = (KS_DEV, agg * agg)
    block = (agg // 2, 2 * agg)
    slot_count = KS_DEV * cols_total
    sums = []
    for stage, parts in enumerate(stages):
        if stage:
            outs = [jax.ShapeDtypeStruct(chunk, BF16 if q else F32) for q in range(cols_total)]
        else:
            outs = [jax.ShapeDtypeStruct((slot_count,) + block, F32)]
        sums = pl.pallas_call(
            partial(sum_kernel, len(parts), not stage, agg_blocks, 12),
            out_shape=outs,
            in_specs=[pl.BlockSpec(memory_space=pl.ANY), HBM] + [VMEM] * (len(parts) + 1 + stage),
            out_specs=[VMEM] * len(outs),
            scratch_shapes=[
                pltpu.SMEM(table.shape, jnp.int32),
                pltpu.SMEM((agg_blocks, agg_blocks, count), jnp.int32),
                pltpu.SemaphoreType.DMA,
                pltpu.SemaphoreType.DMA,
                pltpu.VMEM((1 + len(parts) * fan * per_part, 2 * node, 2 * width), BF16),
            ]
            + [pltpu.VMEM((slot_count,) + block, F32)] * N_ACC,
            compiler_params=pltpu.CompilerParams(vmem_limit_bytes=36 << 20),
            cost_estimate=pl.CostEstimate(
                flops=4 * count * width * node * node, bytes_accessed=10 << 20, transcendentals=0
            ),
        )(table_in, slots, *parts, left, *sums)
    total = sums[0]
    for d in range(1, cols_total):
        total += shift(sums[d], lambda i, d=d: partner(i, d, cols_total)).astype(F32)
    return total.astype(BF16)[None]


def solution(mesh):
    placed = (
        P("row", "col", None, None, None),
        P("row", "col", None),
        P("row", "col", None),
        P(("row", "col"), None, None),
        P("row", "col", None, None, None),
    )

    return jax.shard_map(on_device, mesh=mesh, in_specs=placed, out_specs=P("row", "col", None), check_vma=False)
```
